32 devices in a mesh: seq: 8 (over y, x, core), head: 4 (over z).
Axes of the slice: x: 2, y: 2, z: 4, core: 2. Of those that a mesh axis runs over, the one named last changes fastest.
Arguments:
- queries: bfloat16 [3, 2048, 2048], P(None, 'seq', 'head'), may hold values from -24 to 24
- key_vectors: bfloat16 [4, 2048, 2048], P(None, 'seq', 'head'), may hold values from -24 to 24
- values: bfloat16 [4, 2048, 2048], P(None, 'seq', 'head'), may hold values from -6 to 6
- learn_rates: float32 [3, 2048, 4], P(None, 'seq', 'head'), may hold values from 0.001 to 0.01
- norm_gain: float32 [2048], P('head'), may hold values from 0.1 to 1.9
- out_weight: bfloat16 [2048, 2048], P('head'), may hold values from -0.125 to 0.125
- incoming: float32 [8, 4, 3, 512, 512], P('seq', 'head'), may hold values from -0.25 to 0.25
Outputs:
- mixed_out: bfloat16 [3, 2048, 2048], P(None, 'seq', 'head')
- outgoing: float32 [8, 4, 3, 512, 512], P('seq', 'head')
The draws below stay inside these ranges and needn't reach their ends.
All inputs are finite; a program needn't handle non-finite values.
Results may differ from the reference program's by a relative error of at most 0.013.
The reference program's roundings to bfloat16 on the way count: a program that leaves them out, or rounds other values in their place, can miss the bound.
Values may be sent and summed in bfloat16 or wider, within the bound.
A program may use at most 64 MiB of HBM per device.

```python
import math
import jax
import jax.numpy as jnp
from jax import lax

HEADS = 4
HD = 512
GROUP = 256
TICKS = 3
WIDTH = 2048
SEQ_TOK = 2048
N_SEQ = 8


def paired_draw(key):
    key_raw = jax.random.normal(jax.random.fold_in(key, 101), (TICKS + 1, SEQ_TOK, WIDTH), jnp.float32)
    query_raw = jax.random.normal(jax.random.fold_in(key, 202), (TICKS, SEQ_TOK, WIDTH), jnp.float32)
    return (jnp.clip(key_raw, -24.0, 24.0), jnp.clip(query_raw, -24.0, 24.0))


def draw_queries(key, part):
    return paired_draw(key)[1].astype(jnp.bfloat16)


def draw_key_vectors(key, part):
    return paired_draw(key)[0].astype(jnp.bfloat16)


def levels(rng, shape, cuts, low, largest):
    def one(axis_at, shards_of):
        draws = jax.random.uniform(jax.random.fold_in(jax.random.fold_in(rng, 6), axis_at), (shards_of,), jnp.float32, low / len(cuts), largest / len(cuts))
        return jnp.repeat(jnp.exp(draws), shape[axis_at] // shards_of).reshape((-1,) + (1,) * (len(shape) - axis_at - 1))

    gain = one(*cuts[0])
    for cut in cuts[1:]:
        gain = gain * one(*cut)
    return gain


def centred(rng, dims, deviation, reach, shards=(), dtype=jnp.bfloat16):
    factor_of = levels(rng, dims, shards, -0.22, 0.18) if shards else 1.0
    entries = jax.random.normal(rng, dims, jnp.float32) * deviation * factor_of
    return jnp.minimum(jnp.maximum(entries, -reach), reach).astype(dtype)


def setup_inputs(seed: int = 0) -> dict:
    key_list = jax.random.split(jax.random.key(seed), 8)
    return {
        "queries": draw_queries(jax.random.fold_in(key_list[7], 71), 0),
        "key_vectors": draw_key_vectors(jax.random.fold_in(key_list[7], 71), 0),
        "values": centred(key_list[2], (TICKS + 1, SEQ_TOK, WIDTH), 1.0, 6.0, ((1, 8), (2, 4))),
        "learn_rates": jnp.clip(jnp.exp(math.log(0.01) - 2.30258502 * jax.random.uniform(key_list[3], (TICKS, SEQ_TOK, HEADS), jnp.float32) ** levels(key_list[3], (TICKS, SEQ_TOK, HEADS), ((1, 8), (2, 4)), -0.2, 0.2)), 0.001, 0.01),
        "norm_gain": jnp.clip(1.0 + 0.18 * jax.random.normal(key_list[4], (WIDTH,), jnp.float32), 0.1, 1.9),
        "out_weight": centred(key_list[5], (WIDTH, WIDTH), WIDTH ** -0.5, 0.125, ((0, 4),)),
        "incoming": centred(key_list[6], (N_SEQ, HEADS, 3, HD, HD), HD ** -0.5, 0.25, ((0, 8), (1, 4)), jnp.float32),
    }


def fast_apply(rounded, query_rows):
    first_proj = jnp.dot(query_rows, rounded[0], preferred_element_type=jnp.float32)
    third_proj = jnp.dot(query_rows, rounded[1], preferred_element_type=jnp.float32)
    hidden = (first_proj * jax.nn.sigmoid(first_proj) * third_proj).astype(jnp.bfloat16)
    return jnp.dot(hidden, rounded[2], preferred_element_type=jnp.float32)

def fast_update(fast_state, rounded, key_rows, scaled_values):
    first_proj = jnp.dot(key_rows, rounded[0], preferred_element_type=jnp.float32)
    third_proj = jnp.dot(key_rows, rounded[1], preferred_element_type=jnp.float32)
    gate_sig = jax.nn.sigmoid(first_proj)
    hidden = (first_proj * gate_sig * third_proj).astype(jnp.bfloat16)
    grad_down = jnp.dot(hidden.T, scaled_values, preferred_element_type=jnp.float32)
    back_grad = jnp.dot(scaled_values, rounded[2].T, preferred_element_type=jnp.float32)
    grad_first = (back_grad * third_proj * gate_sig * (1.0 + first_proj * (1.0 - gate_sig))).astype(jnp.bfloat16)
    grad_third = (back_grad * first_proj * gate_sig).astype(jnp.bfloat16)
    grad_one = jnp.dot(key_rows.T, grad_first, preferred_element_type=jnp.float32)
    grad_three = jnp.dot(key_rows.T, grad_third, preferred_element_type=jnp.float32)
    stepped = fast_state + jnp.stack([grad_one, grad_three, grad_down])
    before_sq = lax.optimization_barrier(jnp.mean(fast_state * fast_state, axis=1, keepdims=True))
    after_sq = lax.optimization_barrier(jnp.mean(stepped * stepped, axis=1, keepdims=True))
    return stepped * jnp.sqrt((before_sq + 1e-06) / (after_sq + 1e-06))

def window_attend(query_rows, prior_keys, own_keys, prior_vals, own_vals):
    length = query_rows.shape[0]
    joined_keys = jnp.concatenate([prior_keys, own_keys], axis=0)
    joined_vals = jnp.concatenate([prior_vals, own_vals], axis=0)
    scores = jnp.dot(query_rows, joined_keys.T, preferred_element_type=jnp.float32) * query_rows.shape[1] ** (-0.5)
    query_pos = jnp.arange(length)[:, None] + length
    key_pos = jnp.arange(2 * length)[None, :]
    allowed = (key_pos <= query_pos) & (key_pos > query_pos - length)
    scores = jnp.where(allowed, scores, -1e+30)
    peak = lax.optimization_barrier(jnp.max(scores, axis=1, keepdims=True))
    expo = jnp.exp(scores - peak)
    probs = (expo / lax.optimization_barrier(jnp.sum(expo, axis=1, keepdims=True))).astype(jnp.bfloat16)
    return jnp.dot(probs, joined_vals, preferred_element_type=jnp.float32)

def mix_head(fast_out, attended, gain_row):
    normed = fast_out * lax.rsqrt(lax.optimization_barrier(jnp.mean(fast_out * fast_out, axis=1, keepdims=True)) + 1e-06) * gain_row
    return (attended + normed).astype(jnp.bfloat16)

def one_head(fast_state, query_rows, prior_keys, own_keys, prior_vals, own_vals, rate_rows, gain_row):
    rounded = fast_state.astype(jnp.bfloat16)
    fast_out = fast_apply(rounded, query_rows)
    scaled_values = (rate_rows[:, None] * own_vals.astype(jnp.float32)).astype(jnp.bfloat16)
    updated = fast_update(fast_state, rounded, own_keys, scaled_values)
    attended = window_attend(query_rows, prior_keys, own_keys, prior_vals, own_vals)
    return (mix_head(fast_out, attended, gain_row), updated)

def reference(queries, key_vectors, values, learn_rates, norm_gain, out_weight, incoming):
    query_all = queries.reshape(TICKS, N_SEQ, GROUP, HEADS, HD)
    key_all = key_vectors.reshape(TICKS + 1, N_SEQ, GROUP, HEADS, HD)
    value_all = values.reshape(TICKS + 1, N_SEQ, GROUP, HEADS, HD)
    rate_all = learn_rates.reshape(TICKS, N_SEQ, GROUP, HEADS)
    gains = norm_gain.reshape(HEADS, HD)
    rows_out = out_weight.reshape(HEADS, HD, WIDTH)
    per_head = jax.vmap(one_head, in_axes=(0, 1, 1, 1, 1, 1, 1, 0))

    def one_block(inputs):
        fast_state, query_rows, prior_keys, own_keys, prior_vals, own_vals, rate_rows = inputs
        combined, updated = per_head(fast_state, query_rows, prior_keys, own_keys, prior_vals, own_vals, rate_rows, gains)
        total = jnp.zeros((GROUP, WIDTH), jnp.float32)
        for head_index in range(HEADS):
            partial_value = jnp.dot(combined[head_index], rows_out[head_index], preferred_element_type=jnp.float32).astype(jnp.bfloat16)
            partial_value = lax.optimization_barrier(partial_value)
            total = total + partial_value.astype(jnp.float32)
        return (total.astype(jnp.bfloat16), updated)
    fast_states = incoming
    outputs = []
    for tick_index in range(TICKS):
        mixed, updated = lax.map(one_block, (fast_states, query_all[tick_index], jnp.roll(key_all[tick_index], 1, axis=0), key_all[tick_index + 1], jnp.roll(value_all[tick_index], 1, axis=0), value_all[tick_index + 1], rate_all[tick_index]))
        outputs.append(mixed.reshape(SEQ_TOK, WIDTH))
        if tick_index + 1 < TICKS:
            fast_states = jnp.roll(updated, 1, axis=0)
        else:
            fast_states = updated
    return (jnp.stack(outputs), fast_states)
```

```python
import jax
import jax.numpy as jnp
from jax import lax
from jax.sharding import PartitionSpec as P


def shifted(x, axis, by):
    count = lax.axis_size(axis)
    return lax.ppermute(x, axis, [(i, (i + by) % count) for i in range(count)])


def fast_apply(rounded, query_rows):
    first_proj = jnp.dot(query_rows, rounded[0], preferred_element_type=jnp.float32)
    third_proj = jnp.dot(query_rows, rounded[1], preferred_element_type=jnp.float32)
    hidden = (first_proj * jax.nn.sigmoid(first_proj) * third_proj).astype(jnp.bfloat16)
    return jnp.dot(hidden, rounded[2], preferred_element_type=jnp.float32)


def rescaled(old, grad):
    stepped = old + grad
    before_sq = jnp.mean(old * old, axis=0, keepdims=True)
    after_sq = jnp.mean(stepped * stepped, axis=0, keepdims=True)
    return stepped * jnp.sqrt((before_sq + 1e-06) / (after_sq + 1e-06))


def fast_update(fast_state, rounded, key_rows, scaled_values):
    first_proj = jnp.dot(key_rows, rounded[0], preferred_element_type=jnp.float32)
    third_proj = jnp.dot(key_rows, rounded[1], preferred_element_type=jnp.float32)
    gate_sig = jax.nn.sigmoid(first_proj)
    hidden = (first_proj * gate_sig * third_proj).astype(jnp.bfloat16)
    grad_down = jnp.dot(hidden.T, scaled_values, preferred_element_type=jnp.float32)
    back_grad = jnp.dot(scaled_values, rounded[2].T, preferred_element_type=jnp.float32)
    grad_first = (back_grad * third_proj * gate_sig * (1.0 + first_proj * (1.0 - gate_sig))).astype(
        jnp.bfloat16
    )
    grad_third = (back_grad * first_proj * gate_sig).astype(jnp.bfloat16)
    grad_one = jnp.dot(key_rows.T, grad_first, preferred_element_type=jnp.float32)
    grad_three = jnp.dot(key_rows.T, grad_third, preferred_element_type=jnp.float32)
    grads = (grad_one, grad_three, grad_down)
    return tuple(rescaled(old, grad) for old, grad in zip(fast_state, grads))


def window_attend(query_rows, prior_keys, own_keys, prior_vals, own_vals):
    length = query_rows.shape[0]
    joined_keys = jnp.concatenate([prior_keys, own_keys], axis=0)
    joined_vals = jnp.concatenate([prior_vals, own_vals], axis=0)
    scores = jnp.dot(
        query_rows, joined_keys.T, preferred_element_type=jnp.float32
    ) * query_rows.shape[1] ** (-0.5)
    query_pos = jnp.arange(length)[:, None] + length
    key_pos = jnp.arange(2 * length)[None, :]
    allowed = (key_pos <= query_pos) & (key_pos > query_pos - length)
    scores = jnp.where(allowed, scores, -1e30)
    peak = jnp.max(scores, axis=1, keepdims=True)
    expo = jnp.exp(scores - peak)
    probs = (expo / jnp.sum(expo, axis=1, keepdims=True)).astype(jnp.bfloat16)
    return jnp.dot(probs, joined_vals, preferred_element_type=jnp.float32)


def normed_out(fast_out, gain_row):
    mean_sq = jnp.mean(fast_out * fast_out, axis=1, keepdims=True)
    return fast_out * lax.rsqrt(mean_sq + 1e-06) * gain_row


def scaled(rate_rows, vals):
    return (rate_rows * vals.astype(jnp.float32)).astype(jnp.bfloat16)


def head_sum(partial_value):
    count = lax.axis_size("head")
    me = lax.axis_index("head")
    width = partial_value.shape[1] // count

    def part(of):
        return lax.dynamic_slice_in_dim(partial_value, of * width, width, axis=1)

    total = part(me).astype(jnp.float32)
    for step in range(1, count):
        pairs = [(i, (i + step) % count) for i in range(count)]
        got = lax.ppermute(part((me + step) % count), "head", pairs)
        total = total + got.astype(jnp.float32)
    return total.astype(jnp.bfloat16)


def on_device(queries, key_vectors, values, learn_rates, norm_gain, out_weight, incoming):
    ticks = queries.shape[0]
    last = ticks - 1
    gain_row = norm_gain[None, :]
    near = [shifted((key_vectors[0], values[0]), "seq", 1)]
    ahead = [shifted(queries[1], "seq", -1)]
    near += [shifted((key_vectors[t], values[t]), "seq", 1) for t in (2, 1)]
    near = [near[0], near[2], near[1]]
    rate_near = shifted(learn_rates[1].reshape(1, -1), "seq", 1).reshape(-1, 1)

    def attend(t):
        return window_attend(
            queries[t], near[t][0], key_vectors[t + 1], near[t][1], values[t + 1]
        )

    def mixed(t, normed):
        combined = (attend(t) + normed).astype(jnp.bfloat16)
        partial_value = jnp.dot(combined, out_weight, preferred_element_type=jnp.float32)
        return head_sum(partial_value.astype(jnp.bfloat16))

    state = tuple(incoming[0, 0, i] for i in range(3))
    rounded = tuple(w.astype(jnp.bfloat16) for w in state)
    state = fast_update(state, rounded, key_vectors[1], scaled(learn_rates[0], values[1]))
    sent = tuple(w.astype(jnp.bfloat16) for w in state)
    held = shifted(sent, "seq", last)
    outputs = [mixed(0, normed_out(fast_apply(rounded, queries[0]), gain_row))]
    normed_far = normed_out(fast_apply(sent, ahead[0]), gain_row).astype(jnp.bfloat16)
    normed = shifted(normed_far, "seq", 1).astype(jnp.float32)
    outputs.append(mixed(1, normed))

    state = tuple(w.astype(jnp.float32) for w in held)
    state = fast_update(state, held, near[2][0], scaled(rate_near, near[2][1]))
    rounded = tuple(w.astype(jnp.bfloat16) for w in state)
    outputs.append(mixed(2, normed_out(fast_apply(rounded, queries[2]), gain_row)))
    state = fast_update(state, rounded, key_vectors[3], scaled(learn_rates[2], values[3]))
    return (jnp.stack(outputs), jnp.stack(state)[None, None])


def solution(mesh):
    placed = (
        P(None, "seq", "head"),
        P(None, "seq", "head"),
        P(None, "seq", "head"),
        P(None, "seq", "head"),
        P("head"),
        P("head", None),
        P("seq", "head", None, None, None),
    )
    return jax.shard_map(
        on_device,
        mesh=mesh,
        in_specs=placed,
        out_specs=(P(None, "seq", "head"), P("seq", "head", None, None, None)),
        check_vma=False,
    )
```

```python
import functools

import jax
import jax.numpy as jnp
from jax import lax
from jax.experimental import pallas as pl
from jax.experimental.pallas import tpu as pltpu
from jax.sharding import PartitionSpec as P


F32, BF16 = jnp.float32, jnp.bfloat16


def shifted(x, axis, by):
    count = lax.axis_size(axis)
    return lax.ppermute(x, axis, [(i, (i + by) % count) for i in range(count)])


def dot(a, b, over=(1, 0)):
    return lax.dot_general(a, b, (((over[0],), (over[1],)), ((), ())), preferred_element_type=F32)


def normed_apply(rounded, query_rows, gain_row):
    first_proj = dot(query_rows, rounded[0])
    third_proj = dot(query_rows, rounded[1])
    hidden = (first_proj * jax.nn.sigmoid(first_proj) * third_proj).astype(BF16)
    fast_out = dot(hidden, rounded[2])
    mean_sq = jnp.mean(fast_out * fast_out, axis=1, keepdims=True)
    return fast_out * lax.rsqrt(mean_sq + 1e-06) * gain_row


def fast_update(olds, rounded, key_rows, scaled_values, stores):
    first_proj = dot(key_rows, rounded[0])
    third_proj = dot(key_rows, rounded[1])
    gate_sig = jax.nn.sigmoid(first_proj)
    gated = first_proj * gate_sig

    def put(i, grad):
        old = olds[i]()
        stepped = old + grad
        before_sq = jnp.mean(old * old, axis=0, keepdims=True)
        after_sq = jnp.mean(stepped * stepped, axis=0, keepdims=True)
        stores[i](stepped * jnp.sqrt((before_sq + 1e-06) / (after_sq + 1e-06)))

    hidden = (gated * third_proj).astype(BF16)
    back_grad = dot(scaled_values, rounded[2], (1, 1))
    put(2, dot(hidden, scaled_values, (0, 0)))
    slope = gate_sig * (1.0 + first_proj * (1.0 - gate_sig))
    put(0, dot(key_rows, (back_grad * third_proj * slope).astype(BF16), (0, 0)))
    put(1, dot(key_rows, (back_grad * gated).astype(BF16), (0, 0)))


def attend(query_rows, prior_keys, own_keys, prior_vals, own_vals):
    length, size = query_rows.shape
    row = lax.broadcasted_iota(jnp.int32, (length, length), 0)
    own = lax.broadcasted_iota(jnp.int32, (length, length), 1) <= row
    scores = jnp.where(
        own, dot(query_rows, own_keys, (1, 1)), dot(query_rows, prior_keys, (1, 1))
    ) * size ** (-0.5)
    expo = jnp.exp(scores - jnp.max(scores, axis=1, keepdims=True))
    probs = expo / jnp.sum(expo, axis=1, keepdims=True)
    zero = jnp.zeros_like(probs)
    own_probs = jnp.where(own, probs, zero).astype(BF16)
    prior_probs = jnp.where(own, zero, probs).astype(BF16)
    return dot(own_probs, own_vals) + dot(prior_probs, prior_vals)


def scaled(rate_rows, vals):
    return (rate_rows * vals.astype(F32)).astype(BF16)


def project(combined, weight_ref, keep_ref, send_ref):
    count = lax.axis_size("head")
    me = lax.axis_index("head")
    width = weight_ref.shape[1] // count
    for step in range(count):
        place, slot = divmod(step, 2)
        here = slot + 2 * place
        target = lax.rem(me, 2)
        target = (1 - target if place else target) + 2 * (
            lax.div(me, 2) if slot == 0 else 1 - lax.div(me, 2)
        )
        columns = pl.ds(pl.multiple_of(target * width, 128), width)
        piece = dot(combined, weight_ref[:, columns]).astype(BF16)
        out = send_ref if place else keep_ref
        out[:, slot * width : (slot + 1) * width] = piece


def first_kernel(old_ref, key_ref, val_ref, rate_ref, sent_one, sent_three, sent_down):
    outs = (sent_one, sent_three, sent_down)

    def store(i, x):
        outs[i][...] = x.astype(BF16)

    fast_update(
        [lambda i=i: old_ref[0, 0, i] for i in range(3)],
        [old_ref[0, 0, i].astype(BF16) for i in range(3)],
        key_ref[0],
        scaled(rate_ref[0], val_ref[0]),
        [functools.partial(store, i) for i in range(3)],
    )


def mix_first_kernel(old_ref, q_ref, pk_ref, k_ref, pv_ref, v_ref, gain_ref, w_ref, keep, send):
    rounded = [old_ref[0, 0, i].astype(BF16) for i in range(3)]
    normed = normed_apply(rounded, q_ref[0], gain_ref[...])
    att = attend(q_ref[0], pk_ref[...], k_ref[0], pv_ref[...], v_ref[0])
    project((att + normed).astype(BF16), w_ref, keep, send)


def apply_kernel(one_ref, three_ref, down_ref, q_ref, gain_ref, out_ref):
    rounded = [r[...] for r in (one_ref, three_ref, down_ref)]
    out_ref[...] = normed_apply(rounded, q_ref[...], gain_ref[...]).astype(BF16)


def mix_kernel(normed_ref, q_ref, pk_ref, k_ref, pv_ref, v_ref, w_ref, keep, send):
    att = attend(q_ref[0], pk_ref[...], k_ref[0], pv_ref[...], v_ref[0])
    project((att + normed_ref[...].astype(F32)).astype(BF16), w_ref, keep, send)


def attend_kernel(q_ref, pk_ref, k_ref, pv_ref, v_ref, out_ref):
    out_ref[...] = attend(q_ref[0], pk_ref[...], k_ref[0], pv_ref[...], v_ref[0])


def middle_kernel(
    one_ref, three_ref, down_ref, pk_ref, pv_ref, rate_ref, q_ref, gain_ref, att_ref, w_ref,
    state_ref, keep, send,
):
    held = (one_ref, three_ref, down_ref)

    def store(i, x):
        state_ref[i] = x

    fast_update(
        [lambda i=i: held[i][...].astype(F32) for i in range(3)],
        [r[...] for r in held],
        pk_ref[...],
        scaled(rate_ref[...], pv_ref[...]),
        [functools.partial(store, i) for i in range(3)],
    )
    rounded = [state_ref[i].astype(BF16) for i in range(3)]
    normed = normed_apply(rounded, q_ref[0], gain_ref[...])
    project((att_ref[...] + normed).astype(BF16), w_ref, keep, send)


def last_kernel(old_ref, key_ref, val_ref, rate_ref, out_ref):
    def store(i, x):
        out_ref[0, 0, i] = x

    fast_update(
        [lambda i=i: old_ref[i] for i in range(3)],
        [old_ref[i].astype(BF16) for i in range(3)],
        key_ref[0],
        scaled(rate_ref[0], val_ref[0]),
        [functools.partial(store, i) for i in range(3)],
    )


def whole(x):
    return pl.BlockSpec(x.shape, lambda i: (0,) * len(x.shape))


def at(x, index):
    return pl.BlockSpec((1,) + x.shape[1:], lambda i: (index,) + (0,) * (len(x.shape) - 1))


def call(kernel, args, outs, flops):
    arrays = [a[0] if isinstance(a, tuple) else a for a in args]
    specs = [at(*a) if isinstance(a, tuple) else whole(a) for a in args]
    shapes = [jax.ShapeDtypeStruct(s, t) for s, t in outs]
    got = pl.pallas_call(
        kernel,
        out_shape=shapes,
        grid=(1,),
        in_specs=specs,
        out_specs=[whole(s) for s in shapes],
        compiler_params=pltpu.CompilerParams(vmem_limit_bytes=40 << 20),
        cost_estimate=pl.CostEstimate(flops=flops, bytes_accessed=4 << 20, transcendentals=0),
        name=kernel.__name__,
    )(*arrays)
    return got


def head_sum(keep, send):
    count = lax.axis_size("head")
    width = keep.shape[1] // 2
    got = lax.ppermute(send, "head", [(i, i ^ 1) for i in range(count)])
    pair = keep.astype(F32) + got.astype(F32)
    far = lax.ppermute(pair[:, width:].astype(BF16), "head", [(i, i ^ 2) for i in range(count)])
    return (pair[:, :width] + far.astype(F32)).astype(BF16)


def on_device(queries, key_vectors, values, learn_rates, norm_gain, out_weight, incoming):
    ticks, rows, size = queries.shape
    last = ticks - 1
    unit = 2 * rows * size * size
    gain_row = norm_gain[None, :]
    near = {0: (shifted(key_vectors[0], "seq", 1), shifted(values[0], "seq", 1))}
    ahead = shifted(queries[1], "seq", -1)
    for t in (2, 1):
        near[t] = (shifted(key_vectors[t], "seq", 1), shifted(values[t], "seq", 1))
    rate_near = shifted(learn_rates[1].reshape(1, -1), "seq", 1).reshape(-1, 1)
    half = ((rows, out_weight.shape[1] // 2), BF16)
    weight = ((size, size), BF16)

    def window(t):
        return [(queries, t), near[t][0], (key_vectors, t + 1), near[t][1], (values, t + 1)]

    sent = call(
        first_kernel, [incoming, (key_vectors, 1), (values, 1), (learn_rates, 0)], [weight] * 3, 6 * unit
    )
    held = [shifted(w, "seq", last) for w in (sent[2], sent[0], sent[1])]
    held = (held[1], held[2], held[0])
    (normed_far,) = call(apply_kernel, [*sent, ahead, gain_row], [((rows, size), BF16)], 3 * unit)
    normed = shifted(normed_far, "seq", 1)
    outputs = [
        head_sum(*call(mix_first_kernel, [incoming, *window(0), gain_row, out_weight], [half] * 2, 9 * unit))
    ]
    outputs.append(head_sum(*call(mix_kernel, [normed, *window(1), out_weight], [half] * 2, 6 * unit)))
    (att,) = call(attend_kernel, window(2), [((rows, size), F32)], 2 * unit)
    state, keep, send = call(
        middle_kernel,
        [*held, near[2][0], near[2][1], rate_near, (queries, 2), gain_row, att, out_weight],
        [((3, size, size), F32), half, half],
        13 * unit,
    )
    outputs.append(head_sum(keep, send))
    (outgoing,) = call(
        last_kernel, [state, (key_vectors, 3), (values, 3), (learn_rates, 2)], [(incoming.shape, F32)], 6 * unit
    )
    return (jnp.stack(outputs), outgoing)


def solution(mesh):
    placed = (
        P(None, "seq", "head"),
        P(None, "seq", "head"),
        P(None, "seq", "head"),
        P(None, "seq", "head"),
        P("head"),
        P("head", None),
        P("seq", "head", None, None, None),
    )
    return jax.shard_map(
        on_device,
        mesh=mesh,
        in_specs=placed,
        out_specs=(P(None, "seq", "head"), P("seq", "head", None, None, None)),
        check_vma=False,
    )
```

```python
import functools

import jax
import jax.numpy as jnp
from jax import lax
from jax.experimental import pallas as pl
from jax.experimental.pallas import tpu as pltpu
from jax.sharding import PartitionSpec as P


F32, BF16 = jnp.float32, jnp.bfloat16


def shifted(x, axis, by):
    count = lax.axis_size(axis)
    return lax.ppermute(x, axis, [(i, (i + by) % count) for i in range(count)])


def dot(a, b, over=(1, 0)):
    return lax.dot_general(a, b, (((over[0],), (over[1],)), ((), ())), preferred_element_type=F32)


def normed_apply(rounded, query_rows, gain_row):
    first_proj = dot(query_rows, rounded[0])
    third_proj = dot(query_rows, rounded[1])
    hidden = (first_proj * jax.nn.sigmoid(first_proj) * third_proj).astype(BF16)
    fast_out = dot(hidden, rounded[2])
    mean_sq = jnp.mean(fast_out * fast_out, axis=1, keepdims=True)
    return fast_out * lax.rsqrt(mean_sq + 1e-06) * gain_row


def fast_update(olds, rounded, key_rows, scaled_values, stores):
    first_proj = dot(key_rows, rounded[0])
    third_proj = dot(key_rows, rounded[1])
    gate_sig = jax.nn.sigmoid(first_proj)
    gated = first_proj * gate_sig

    def put(i, grad):
        old = olds[i]()
        stepped = old + grad
        before_sq = jnp.mean(old * old, axis=0, keepdims=True)
        after_sq = jnp.mean(stepped * stepped, axis=0, keepdims=True)
        stores[i](stepped * jnp.sqrt((before_sq + 1e-06) / (after_sq + 1e-06)))

    hidden = (gated * third_proj).astype(BF16)
    back_grad = dot(scaled_values, rounded[2], (1, 1))
    put(2, dot(hidden, scaled_values, (0, 0)))
    slope = gate_sig * (1.0 + first_proj * (1.0 - gate_sig))
    put(0, dot(key_rows, (back_grad * third_proj * slope).astype(BF16), (0, 0)))
    put(1, dot(key_rows, (back_grad * gated).astype(BF16), (0, 0)))


def attend(query_rows, prior_keys, own_keys, prior_vals, own_vals):
    length, size = query_rows.shape
    row = lax.broadcasted_iota(jnp.int32, (length, length), 0)
    own = lax.broadcasted_iota(jnp.int32, (length, length), 1) <= row
    scores = jnp.where(
        own, dot(query_rows, own_keys, (1, 1)), dot(query_rows, prior_keys, (1, 1))
    ) * size ** (-0.5)
    expo = jnp.exp(scores - jnp.max(scores, axis=1, keepdims=True))
    probs = expo / jnp.sum(expo, axis=1, keepdims=True)
    zero = jnp.zeros_like(probs)
    own_probs = jnp.where(own, probs, zero).astype(BF16)
    prior_probs = jnp.where(own, zero, probs).astype(BF16)
    return dot(own_probs, own_vals) + dot(prior_probs, prior_vals)


def scaled(rate_rows, vals):
    return (rate_rows * vals.astype(F32)).astype(BF16)


def project(combined, weight_ref, keep_ref, send_ref):
    count = lax.axis_size("head")
    me = lax.axis_index("head")
    width = weight_ref.shape[1] // count
    for step in range(count):
        place, slot = divmod(step, 2)
        target = lax.rem(me, 2)
        target = (1 - target if place else target) + 2 * (
            lax.div(me, 2) if slot == 0 else 1 - lax.div(me, 2)
        )
        columns = pl.ds(pl.multiple_of(target * width, 128), width)
        piece = dot(combined, weight_ref[:, columns]).astype(BF16)
        out = send_ref if place else keep_ref
        out[:, slot * width : (slot + 1) * width] = piece


def split_kernel(q_ref, key0, key1, key2, val0, val1, val2, q_out, near0, near1, near2):
    q_out[...] = q_ref[0]
    for out, k_ref, v_ref in ((near0, key0, val0), (near1, key1, val1), (near2, key2, val2)):
        out[0] = k_ref[0]
        out[1] = v_ref[0]


def first_kernel(old_ref, key_ref, val_ref, rate_ref, sent_ref):
    def store(i, x):
        sent_ref[i] = x.astype(BF16)

    fast_update(
        [lambda i=i: old_ref[0, 0, i] for i in range(3)],
        [old_ref[0, 0, i].astype(BF16) for i in range(3)],
        key_ref[0],
        scaled(rate_ref[0], val_ref[0]),
        [functools.partial(store, i) for i in range(3)],
    )


def window_of(near_ref, q_ref, k_ref, v_ref):
    return attend(q_ref[0], near_ref[0], k_ref[0], near_ref[1], v_ref[0])


def mix_first_kernel(old_ref, near_ref, q_ref, k_ref, v_ref, gain_ref, w_ref, keep, send):
    rounded = [old_ref[0, 0, i].astype(BF16) for i in range(3)]
    normed = normed_apply(rounded, q_ref[0], gain_ref[...])
    att = window_of(near_ref, q_ref, k_ref, v_ref)
    project((att + normed).astype(BF16), w_ref, keep, send)


def apply_kernel(held_ref, q_ref, gain_ref, out_ref):
    rounded = [held_ref[i] for i in range(3)]
    out_ref[...] = normed_apply(rounded, q_ref[...], gain_ref[...]).astype(BF16)


def mix_kernel(normed_ref, near_ref, q_ref, k_ref, v_ref, w_ref, keep, send):
    att = window_of(near_ref, q_ref, k_ref, v_ref)
    project((att + normed_ref[...].astype(F32)).astype(BF16), w_ref, keep, send)


def attend_kernel(near_ref, q_ref, k_ref, v_ref, out_ref):
    out_ref[...] = window_of(near_ref, q_ref, k_ref, v_ref)


def middle_kernel(
    held_ref, near_ref, rate_ref, q_ref, gain_ref, att_ref, w_ref, state_ref, *halves
):
    def store(i, x):
        state_ref[i] = x

    fast_update(
        [lambda i=i: held_ref[i].astype(F32) for i in range(3)],
        [held_ref[i] for i in range(3)],
        near_ref[0],
        scaled(rate_ref[...], near_ref[1]),
        [functools.partial(store, i) for i in range(3)],
    )
    rounded = [state_ref[i].astype(BF16) for i in range(3)]
    normed = normed_apply(rounded, q_ref[0], gain_ref[...])
    combined = (att_ref[...] + normed).astype(BF16)
    rows = halves[0].shape[0]
    for at_row in range(0, combined.shape[0], rows):
        keep, send = halves[2 * (at_row // rows) :][:2]
        project(combined[at_row : at_row + rows], w_ref, keep, send)


def last_kernel(old_ref, key_ref, val_ref, rate_ref, out_ref):
    def store(i, x):
        out_ref[0, 0, i] = x

    fast_update(
        [lambda i=i: old_ref[i] for i in range(3)],
        [old_ref[i].astype(BF16) for i in range(3)],
        key_ref[0],
        scaled(rate_ref[0], val_ref[0]),
        [functools.partial(store, i) for i in range(3)],
    )


def whole(x):
    return pl.BlockSpec(x.shape, lambda i: (0,) * len(x.shape))


def at(x, index):
    return pl.BlockSpec((1,) + x.shape[1:], lambda i: (index,) + (0,) * (len(x.shape) - 1))


def call(kernel, args, outs, flops):
    arrays = [a[0] if isinstance(a, tuple) else a for a in args]
    specs = [at(*a) if isinstance(a, tuple) else whole(a) for a in args]
    shapes = [jax.ShapeDtypeStruct(s, t) for s, t in outs]
    got = pl.pallas_call(
        kernel,
        out_shape=shapes,
        grid=(1,),
        in_specs=specs,
        out_specs=[whole(s) for s in shapes],
        compiler_params=pltpu.CompilerParams(vmem_limit_bytes=40 << 20),
        cost_estimate=pl.CostEstimate(flops=flops, bytes_accessed=4 << 20, transcendentals=0),
    )(*arrays)
    return got


def pair_sum(keep, send):
    count = lax.axis_size("head")
    got = lax.ppermute(send, "head", [(i, i ^ 1) for i in range(count)])
    pair = keep.astype(F32) + got.astype(F32)
    width = keep.shape[1] // 2
    return pair[:, :width], pair[:, width:].astype(BF16)


def last_sum(own, far):
    count = lax.axis_size("head")
    got = lax.ppermute(far, "head", [(i, i ^ 2) for i in range(count)])
    return (own + got.astype(F32)).astype(BF16)


def layer(queries, key_vectors, values, learn_rates, norm_gain, out_weight, incoming):
    ticks, rows, size = queries.shape
    last = ticks - 1
    unit = 2 * rows * size * size
    gain_row = norm_gain[None, :]
    wide = out_weight.shape[1] // 2
    half, quarter = ((rows, wide), BF16), ((rows // 2, wide), BF16)
    both = ((2, rows, size), BF16)
    block = ((rows, size), BF16)

    rate_near = shifted(learn_rates[1].reshape(1, -1), "seq", 1).reshape(-1, 1)
    ahead, near0, near1, near2 = call(
        split_kernel,
        [(queries, 1)] + [(key_vectors, t) for t in range(3)] + [(values, t) for t in range(3)],
        [block, both, both, both],
        0,
    )
    ahead = shifted(ahead, "seq", -1)
    near0 = shifted(near0, "seq", 1)
    near1 = shifted(near1, "seq", 1)

    def window(t):
        return [(queries, t), (key_vectors, t + 1), (values, t + 1)]

    (sent,) = call(
        first_kernel,
        [incoming, (key_vectors, 1), (values, 1), (learn_rates, 0)],
        [((3, size, size), BF16)],
        6 * unit,
    )
    (normed_far,) = call(apply_kernel, [sent, ahead, gain_row], [block], 3 * unit)
    normed = shifted(normed_far, "seq", 1)
    near2 = shifted(near2, "seq", 1)
    held = shifted(sent, "seq", last)
    near0, rate_near = lax.optimization_barrier((near0, rate_near))
    sums = [
        pair_sum(
            *call(mix_first_kernel, [incoming, near0, *window(0), gain_row, out_weight], [half] * 2, 9 * unit)
        )
    ]
    sums.append(pair_sum(*call(mix_kernel, [normed, near1, *window(1), out_weight], [half] * 2, 6 * unit)))
    (att,) = call(attend_kernel, [near2, *window(2)], [((rows, size), F32)], 2 * unit)
    state, *halves = call(
        middle_kernel,
        [held, near2, rate_near, (queries, 2), gain_row, att, out_weight],
        [((3, size, size), F32)] + [quarter] * 4,
        13 * unit,
    )
    outputs = [last_sum(*pair) for pair in sums]
    lower = last_sum(*pair_sum(*halves[:2]))
    upper = last_sum(*pair_sum(*halves[2:]))
    outputs.append(jnp.concatenate([lower, upper], axis=0))
    (outgoing,) = call(
        last_kernel, [state, (key_vectors, 3), (values, 3), (learn_rates, 2)], [(incoming.shape, F32)], 6 * unit
    )
    return (jnp.stack(outputs), outgoing)


def solution(mesh):
    placed = (
        P(None, "seq", "head"),
        P(None, "seq", "head"),
        P(None, "seq", "head"),
        P(None, "seq", "head"),
        P("head"),
        P("head", None),
        P("seq", "head", None, None, None),
    )
    return jax.shard_map(
        layer,
        mesh=mesh,
        in_specs=placed,
        out_specs=(P(None, "seq", "head"), P("seq", "head", None, None, None)),
        check_vma=False,
    )
```

```python
import functools

import jax
import jax.numpy as jnp
from jax import lax
from jax.experimental import pallas as pl
from jax.experimental.pallas import tpu as pltpu
from jax.sharding import PartitionSpec as P


F32, BF16 = jnp.float32, jnp.bfloat16


def shifted(x, axis, by):
    count = lax.axis_size(axis)
    return lax.ppermute(x, axis, [(i, (i + by) % count) for i in range(count)])


def dot(a, b, over=(1, 0)):
    return lax.dot_general(a, b, (((over[0],), (over[1],)), ((), ())), preferred_element_type=F32)


def normed_apply(rounded, query_rows, gain_row):
    first_proj = dot(query_rows, rounded[0])
    third_proj = dot(query_rows, rounded[1])
    hidden = (first_proj * jax.nn.sigmoid(first_proj) * third_proj).astype(BF16)
    fast_out = dot(hidden, rounded[2])
    mean_sq = jnp.mean(fast_out * fast_out, axis=1, keepdims=True)
    return fast_out * lax.rsqrt(mean_sq + 1e-06) * gain_row


def fast_update(olds, rounded, key_rows, scaled_values, stores):
    first_proj = dot(key_rows, rounded[0])
    third_proj = dot(key_rows, rounded[1])
    gate_sig = jax.nn.sigmoid(first_proj)
    gated = first_proj * gate_sig

    def put(i, grad):
        old = olds[i]()
        stepped = old + grad
        before_sq = jnp.mean(old * old, axis=0, keepdims=True)
        after_sq = jnp.mean(stepped * stepped, axis=0, keepdims=True)
        stores[i](stepped * jnp.sqrt((before_sq + 1e-06) / (after_sq + 1e-06)))

    hidden = (gated * third_proj).astype(BF16)
    back_grad = dot(scaled_values, rounded[2], (1, 1))
    put(2, dot(hidden, scaled_values, (0, 0)))
    slope = gate_sig * (1.0 + first_proj * (1.0 - gate_sig))
    put(0, dot(key_rows, (back_grad * third_proj * slope).astype(BF16), (0, 0)))
    put(1, dot(key_rows, (back_grad * gated).astype(BF16), (0, 0)))


def attend(query_rows, prior_keys, own_keys, prior_vals, own_vals):
    length, size = query_rows.shape
    row = lax.broadcasted_iota(jnp.int32, (length, length), 0)
    own = lax.broadcasted_iota(jnp.int32, (length, length), 1) <= row
    scores = jnp.where(
        own, dot(query_rows, own_keys, (1, 1)), dot(query_rows, prior_keys, (1, 1))
    ) * size ** (-0.5)
    expo = jnp.exp(scores - jnp.max(scores, axis=1, keepdims=True))
    probs = expo / jnp.sum(expo, axis=1, keepdims=True)
    zero = jnp.zeros_like(probs)
    own_probs = jnp.where(own, probs, zero).astype(BF16)
    prior_probs = jnp.where(own, zero, probs).astype(BF16)
    return dot(own_probs, own_vals) + dot(prior_probs, prior_vals)


def scaled(rate_rows, vals):
    return (rate_rows * vals.astype(F32)).astype(BF16)


def project(combined, weight_ref, keep_ref, send_ref):
    count = lax.axis_size("head")
    me = lax.axis_index("head")
    width = weight_ref.shape[1] // count
    for step in range(count):
        place, slot = divmod(step, 2)
        target = lax.rem(me, 2)
        target = (1 - target if place else target) + 2 * (
            lax.div(me, 2) if slot == 0 else 1 - lax.div(me, 2)
        )
        columns = pl.ds(pl.multiple_of(target * width, 128), width)
        piece = dot(combined, weight_ref[:, columns]).astype(BF16)
        out = send_ref if place else keep_ref
        out[:, slot * width : (slot + 1) * width] = piece


def split_first_kernel(q_ref, key0, val0, q_out, near0):
    q_out[...] = q_ref[0]
    near0[0] = key0[0]
    near0[1] = val0[0]


def split_kernel(key1, key2, val1, val2, near1, near2):
    for out, k_ref, v_ref in ((near1, key1, val1), (near2, key2, val2)):
        out[0] = k_ref[0]
        out[1] = v_ref[0]


def first_kernel(old_ref, key_ref, val_ref, rate_ref, sent_ref):
    def store(i, x):
        sent_ref[i] = x.astype(BF16)

    fast_update(
        [lambda i=i: old_ref[0, 0, i] for i in range(3)],
        [old_ref[0, 0, i].astype(BF16) for i in range(3)],
        key_ref[0],
        scaled(rate_ref[0], val_ref[0]),
        [functools.partial(store, i) for i in range(3)],
    )


def window_of(near_ref, q_ref, k_ref, v_ref):
    return attend(q_ref[0], near_ref[0], k_ref[0], near_ref[1], v_ref[0])


def mix_first_kernel(old_ref, near_ref, q_ref, k_ref, v_ref, gain_ref, w_ref, keep, send):
    rounded = [old_ref[0, 0, i].astype(BF16) for i in range(3)]
    normed = normed_apply(rounded, q_ref[0], gain_ref[...])
    att = window_of(near_ref, q_ref, k_ref, v_ref)
    project((att + normed).astype(BF16), w_ref, keep, send)


def apply_kernel(held_ref, q_ref, gain_ref, out_ref):
    rounded = [held_ref[i] for i in range(3)]
    out_ref[...] = normed_apply(rounded, q_ref[...], gain_ref[...]).astype(BF16)


def mix_kernel(normed_ref, near_ref, q_ref, k_ref, v_ref, w_ref, keep, send):
    att = window_of(near_ref, q_ref, k_ref, v_ref)
    project((att + normed_ref[...].astype(F32)).astype(BF16), w_ref, keep, send)


def attend_kernel(near_ref, q_ref, k_ref, v_ref, out_ref):
    out_ref[...] = window_of(near_ref, q_ref, k_ref, v_ref)


def middle_kernel(
    held_ref, near_ref, rate_ref, q_ref, gain_ref, att_ref, w_ref, state_ref, *halves
):
    def store(i, x):
        state_ref[i] = x

    fast_update(
        [lambda i=i: held_ref[i].astype(F32) for i in range(3)],
        [held_ref[i] for i in range(3)],
        near_ref[0],
        scaled(rate_ref[...], near_ref[1]),
        [functools.partial(store, i) for i in range(3)],
    )
    rounded = [state_ref[i].astype(BF16) for i in range(3)]
    normed = normed_apply(rounded, q_ref[0], gain_ref[...])
    combined = (att_ref[...] + normed).astype(BF16)
    at_row = 0
    for keep, send in zip(halves[::2], halves[1::2]):
        rows = keep.shape[0]
        project(combined[at_row : at_row + rows], w_ref, keep, send)
        at_row += rows


def last_kernel(old_ref, key_ref, val_ref, rate_ref, out_ref):
    def store(i, x):
        out_ref[0, 0, i] = x

    fast_update(
        [lambda i=i: old_ref[i] for i in range(3)],
        [old_ref[i].astype(BF16) for i in range(3)],
        key_ref[0],
        scaled(rate_ref[0], val_ref[0]),
        [functools.partial(store, i) for i in range(3)],
    )


def whole(x):
    return pl.BlockSpec(x.shape, lambda i: (0,) * len(x.shape))


def at(x, index):
    return pl.BlockSpec((1,) + x.shape[1:], lambda i: (index,) + (0,) * (len(x.shape) - 1))


def call(kernel, args, outs, flops, vmem=40 << 20):
    arrays = [a[0] if isinstance(a, tuple) else a for a in args]
    specs = [at(*a) if isinstance(a, tuple) else whole(a) for a in args]
    shapes = [jax.ShapeDtypeStruct(s, t) for s, t in outs]
    got = pl.pallas_call(
        kernel,
        out_shape=shapes,
        grid=(1,),
        in_specs=specs,
        out_specs=[whole(s) for s in shapes],
        compiler_params=pltpu.CompilerParams(vmem_limit_bytes=vmem),
        cost_estimate=pl.CostEstimate(flops=flops, bytes_accessed=4 << 20, transcendentals=0),
    )(*arrays)
    return got


def pair_sum(keep, send):
    count = lax.axis_size("head")
    got = lax.ppermute(send, "head", [(i, i ^ 1) for i in range(count)])
    pair = keep.astype(F32) + got.astype(F32)
    width = keep.shape[1] // 2
    return pair[:, :width], pair[:, width:].astype(BF16)


def last_sum(own, far):
    count = lax.axis_size("head")
    got = lax.ppermute(far, "head", [(i, i ^ 2) for i in range(count)])
    return (own + got.astype(F32)).astype(BF16)


def layer(queries, key_vectors, values, learn_rates, norm_gain, out_weight, incoming):
    ticks, rows, size = queries.shape
    last = ticks - 1
    unit = 2 * rows * size * size
    gain_row = norm_gain[None, :]
    wide = out_weight.shape[1] // 2
    half = ((rows, wide), BF16)
    chunks = (3 * rows // 8, 3 * rows // 8, rows // 4)
    both = ((2, rows, size), BF16)
    block = ((rows, size), BF16)

    rate_near = shifted(learn_rates[1].reshape(1, -1), "seq", 1).reshape(-1, 1)
    ahead, near0 = call(
        split_first_kernel, [(queries, 1), (key_vectors, 0), (values, 0)], [block, both], 0, 60 << 20
    )
    near1, near2 = call(
        split_kernel,
        [(key_vectors, 1), (key_vectors, 2), (values, 1), (values, 2)],
        [both, both],
        0,
        60 << 20,
    )
    ahead = shifted(ahead, "seq", -1)
    near0 = shifted(near0, "seq", 1)
    near1 = shifted(near1, "seq", 1)

    def window(t):
        return [(queries, t), (key_vectors, t + 1), (values, t + 1)]

    (sent,) = call(
        first_kernel,
        [incoming, (key_vectors, 1), (values, 1), (learn_rates, 0)],
        [((3, size, size), BF16)],
        6 * unit,
    )
    (normed_far,) = call(apply_kernel, [sent, ahead, gain_row], [block], 3 * unit)
    normed = shifted(normed_far, "seq", 1)
    near2 = shifted(near2, "seq", 1)
    held = shifted(sent, "seq", last)
    near0, rate_near = lax.optimization_barrier((near0, rate_near))
    sums = [
        pair_sum(
            *call(mix_first_kernel, [incoming, near0, *window(0), gain_row, out_weight], [half] * 2, 9 * unit),
        )
    ]
    sums.append(pair_sum(*call(mix_kernel, [normed, near1, *window(1), out_weight], [half] * 2, 6 * unit)))
    (att,) = call(attend_kernel, [near2, *window(2)], [((rows, size), F32)], 2 * unit)
    state, *halves = call(
        middle_kernel,
        [held, near2, rate_near, (queries, 2), gain_row, att, out_weight],
        [((3, size, size), F32)] + [((c, wide), BF16) for c in chunks for _ in range(2)],
        13 * unit,
    )
    (outgoing,) = call(
        last_kernel,
        [state, (key_vectors, 3), (values, 3), (learn_rates, 2)],
        [(incoming.shape, F32)],
        6 * unit,
    )
    own, outgoing = lax.optimization_barrier((sums[1][0], outgoing))
    sums[1] = (own, sums[1][1])
    pieces = [(t, 0, last_sum(*pair)) for t, pair in enumerate(sums)]
    at_row = 0
    for i, chunk in enumerate(chunks):
        pair = pair_sum(*halves[2 * i : 2 * i + 2])
        pieces.append((last, at_row, last_sum(*pair)))
        at_row += chunk
    out = jnp.zeros(queries.shape, BF16)
    for t, row, piece in pieces:
        out = lax.dynamic_update_slice(out, piece[None], (t, row, 0))
    return (out, outgoing)


def solution(mesh):
    placed = (
        P(None, "seq", "head"),
        P(None, "seq", "head"),
        P(None, "seq", "head"),
        P(None, "seq", "head"),
        P("head"),
        P("head", None),
        P("seq", "head", None, None, None),
    )
    return jax.shard_map(
        layer,
        mesh=mesh,
        in_specs=placed,
        out_specs=(P(None, "seq", "head"), P("seq", "head", None, None, None)),
        check_vma=False,
    )
```
